32 devices in a mesh: dp: 8 (over y, x, core), fsdp: 4 (over z).
Axes of the slice: x: 2, y: 2, z: 4, core: 2. Of those that a mesh axis runs over, the one named last changes fastest.
Arguments:
- tokens: bfloat16 [4096, 1152], P(('dp', 'fsdp')), may hold values from -6 to 6
- cotangent: bfloat16 [4096, 1152], P(('dp', 'fsdp')), may hold values from -6 to 6
- seq_ids: int32 [4096], P(('dp', 'fsdp')), may hold values from -1 to 127, as said below
- w_query: bfloat16 [1152, 1024], P(('dp', 'fsdp')), may hold values from -0.1875 to 0.1875
- w_key: bfloat16 [1152, 256], P(('dp', 'fsdp')), may hold values from -0.1875 to 0.1875
- w_value: bfloat16 [1152, 256], P(('dp', 'fsdp')), may hold values from -0.1875 to 0.1875
- w_output: bfloat16 [1024, 1152], P(('dp', 'fsdp')), may hold values from -0.1875 to 0.1875
- ffn_rows: bfloat16 [6912, 3456], P(('dp', 'fsdp')), may hold values from -0.1875 to 0.1875
- gain_attn_pre: bfloat16 [1152], P(('dp', 'fsdp')), may hold values from 0.099609375 to 1.8984375
- gain_attn_post: bfloat16 [1152], P(('dp', 'fsdp')), may hold values from 0.099609375 to 1.8984375
- gain_query: bfloat16 [256], P(('dp', 'fsdp')), may hold values from 0.099609375 to 1.8984375
- gain_key: bfloat16 [256], P(('dp', 'fsdp')), may hold values from 0.099609375 to 1.8984375
- gain_ffn_pre: bfloat16 [1152], P(('dp', 'fsdp')), may hold values from 0.099609375 to 1.8984375
- gain_ffn_post: bfloat16 [1152], P(('dp', 'fsdp')), may hold values from 0.099609375 to 1.8984375
Outputs:
- activations: bfloat16 [4096, 1152], P(('dp', 'fsdp'))
- token_grad: float32 [4096, 1152], P(('dp', 'fsdp'))
- grad_query: float32 [1152, 1024], P(('dp', 'fsdp'))
- grad_key: float32 [1152, 256], P(('dp', 'fsdp'))
- grad_value: float32 [1152, 256], P(('dp', 'fsdp'))
- grad_output: float32 [1024, 1152], P(('dp', 'fsdp'))
- grad_ffn_rows: float32 [6912, 3456], P(('dp', 'fsdp'))
- grad_attn_pre: float32 [1152], P(('dp', 'fsdp'))
- grad_attn_post: float32 [1152], P(('dp', 'fsdp'))
- grad_query_gain: float32 [256], P(('dp', 'fsdp'))
- grad_key_gain: float32 [256], P(('dp', 'fsdp'))
- grad_ffn_pre: float32 [1152], P(('dp', 'fsdp'))
- grad_ffn_post: float32 [1152], P(('dp', 'fsdp'))
The draws below stay inside these ranges and needn't reach their ends.
Inputs may be any that keep to these rules, and one draw needn't show every extreme that they name: `seq_ids`: in each block of 128 rows the used slots come first and carry sequence numbers 0, 1, 2, ... in order; the rest are -1. A sequence has at most 96 rows and some sequence has exactly 96; every block has 96 or more used slots, some block is full, and some block holds 128 sequences of one row.
All inputs are finite; a program needn't handle non-finite values.
Results may differ from the reference program's by a relative error of at most 0.015.
Values may be sent and summed in bfloat16 or wider, within the bound.
No kernel may reach another device: no remote copies, remote signals or barrier semaphores. Data moves between devices by JAX's collectives and lax.ppermute only.
A program may use at most 448 MiB of HBM per device.

```python
import math
import jax
import jax.numpy as jnp
from jax import lax

D = 1152
HEAD = 256
FF = 6912
CAP = 128
HD = 1024
MAXLEN = 96
ROWS = 4096


def draw_seq_ids(key, part):
    devices = ROWS // CAP
    key_live, key_full, key_len, key_ones = jax.random.split(key, 4)
    shifts = jax.random.randint(key_live, (devices,), 0, 3)
    live = jnp.where(shifts == 0, CAP, jnp.where(shifts == 1, CAP - CAP // 8, CAP - CAP // 4))
    full_dev = jax.random.randint(key_full, (), 0, devices)
    ones_dev = (full_dev + 1 + jax.random.randint(key_ones, (), 0, devices - 1)) % devices
    dev_index = jnp.arange(devices, dtype=jnp.int32)
    live = jnp.where((dev_index == full_dev) | (dev_index == ones_dev), CAP, live).astype(jnp.int32)
    lengths = jax.random.randint(key_len, (devices, CAP), 1, MAXLEN + 1)
    column = jnp.arange(CAP, dtype=jnp.int32)
    lengths = jnp.where((dev_index[:, None] == full_dev) & (column[None, :] == 0), MAXLEN, lengths)
    lengths = jnp.where(dev_index[:, None] == ones_dev, 1, lengths).astype(jnp.int32)
    starts = jnp.cumsum(lengths, axis=1) - lengths
    segment = jnp.sum(jnp.where(starts[:, None, :] <= column[None, :, None], 1, 0), axis=2) - 1
    segment = jnp.where(column[None, :] < live[:, None], segment, -1)
    return segment.reshape(ROWS).astype(jnp.int32)


def block_scale(stream_key, extent, cuts, least, high):
    def one(axis_at, blocks):
        steps = jax.random.uniform(jax.random.fold_in(jax.random.fold_in(stream_key, 6), axis_at), (blocks,), jnp.float32, least / len(cuts), high / len(cuts))
        return jnp.repeat(jnp.exp(steps), extent[axis_at] // blocks).reshape((-1,) + (1,) * (len(extent) - axis_at - 1))

    loudness = one(*cuts[0])
    for cut in cuts[1:]:
        loudness = loudness * one(*cut)
    return loudness


def noise(own_key, extent, scale, bound, shards=(), kind=jnp.bfloat16):
    loudness = block_scale(own_key, extent, shards, -0.22, 0.18) if shards else 1.0
    drawn = jax.random.normal(own_key, extent, jnp.float32) * scale * loudness
    return jnp.minimum(jnp.maximum(drawn, -bound), bound).astype(kind)


def setup_inputs(seed: int = 0) -> dict:
    splits = jax.random.split(jax.random.key(seed), 15)
    return {
        "tokens": noise(splits[0], (ROWS, D), 1.0, 6.0, ((0, 32),)),
        "cotangent": noise(splits[1], (ROWS, D), 1.0, 6.0, ((0, 32),)),
        "seq_ids": draw_seq_ids(jax.random.fold_in(splits[14], 71), 0),
        "w_query": noise(splits[3], (D, HD), D ** -0.5, 0.1875, ((0, 32),)),
        "w_key": noise(splits[4], (D, HEAD), D ** -0.5, 0.1875, ((0, 32),)),
        "w_value": noise(splits[5], (D, HEAD), D ** -0.5, 0.1875, ((0, 32),)),
        "w_output": noise(splits[6], (HD, D), HD ** -0.5, 0.1875, ((0, 32),)),
        "ffn_rows": noise(splits[7], (FF, 3 * D), D ** -0.5, 0.1875, ((0, 32),)),
        "gain_attn_pre": jnp.clip(1.0 + 0.18 * jax.random.normal(splits[8], (D,), jnp.float32), 0.099609375, 1.8984375).astype(jnp.bfloat16),
        "gain_attn_post": jnp.clip(1.0 + 0.18 * jax.random.normal(splits[9], (D,), jnp.float32), 0.099609375, 1.8984375).astype(jnp.bfloat16),
        "gain_query": jnp.clip(1.0 + 0.18 * jax.random.normal(splits[10], (HEAD,), jnp.float32), 0.099609375, 1.8984375).astype(jnp.bfloat16),
        "gain_key": jnp.clip(1.0 + 0.18 * jax.random.normal(splits[11], (HEAD,), jnp.float32), 0.099609375, 1.8984375).astype(jnp.bfloat16),
        "gain_ffn_pre": jnp.clip(1.0 + 0.18 * jax.random.normal(splits[12], (D,), jnp.float32), 0.099609375, 1.8984375).astype(jnp.bfloat16),
        "gain_ffn_post": jnp.clip(1.0 + 0.18 * jax.random.normal(splits[13], (D,), jnp.float32), 0.099609375, 1.8984375).astype(jnp.bfloat16),
    }


EPS = 1e-06
SCALE = 0.0625
BASE = 10000.0
CUBIC = 0.044715
ROOT_TERM = 0.7978845608028654

def normalize(values):
    factor = lax.rsqrt(lax.optimization_barrier(jnp.mean(values * values, axis=-1, keepdims=True)) + EPS)
    return (values * factor, factor)

def norm_back(incoming, unit, factor):
    return factor * (incoming - unit * lax.optimization_barrier(jnp.mean(incoming * unit, axis=-1, keepdims=True)))

def gelu_pair(values):
    tangent = jnp.tanh(ROOT_TERM * (values + CUBIC * values * values * values))
    result = 0.5 * values * (1.0 + tangent)
    slope = 0.5 * (1.0 + tangent) + 0.5 * values * (1.0 - tangent * tangent) * ROOT_TERM * (1.0 + 3.0 * CUBIC * values * values)
    return (result, slope)

def rotary(values, position, direction):
    half = values.shape[-1] // 2
    ladder = jnp.arange(half, dtype=jnp.float32) * (2.0 / values.shape[-1])
    freq = jnp.power(jnp.float32(BASE), -ladder)
    angle = position.astype(jnp.float32)[:, None] * freq[None, :]
    cosine = jnp.cos(angle)[:, None, :]
    sine = direction * jnp.sin(angle)[:, None, :]
    first = values[..., :half]
    second = values[..., half:]
    return jnp.concatenate([first * cosine - second * sine, second * cosine + first * sine], axis=-1)

def layout_of(labels):
    count = labels.shape[0]
    index = jnp.arange(count, dtype=jnp.int32)
    same = labels[:, None] == labels[None, :]
    earlier = index[None, :] < index[:, None]
    position = lax.optimization_barrier(jnp.sum(jnp.where(same & earlier, 1, 0), axis=1)).astype(jnp.int32)
    allowed = same & (index[None, :] <= index[:, None])
    return (position, allowed)

def product(left, right):
    return jnp.dot(left, right, preferred_element_type=jnp.float32)

def cross_rows(left, right):
    return lax.dot_general(left, right, (((0,), (0,)), ((), ())), preferred_element_type=jnp.float32)

def cross_cols(left, right):
    return lax.dot_general(left, right, (((1,), (1,)), ((), ())), preferred_element_type=jnp.float32)

def batched(form, left, right):
    return jnp.einsum(form, left.astype(jnp.float32), right.astype(jnp.float32))

def attention_forward(attn_in, query_full, key_full, value_full, gain_q, gain_k, position, allowed):
    count = attn_in.shape[0]
    head_size = key_full.shape[1]
    heads = query_full.shape[1] // head_size
    queries = product(attn_in, query_full).reshape(count, heads, head_size)
    key_rows = product(attn_in, key_full)[:, None, :]
    value_rows = product(attn_in, value_full).astype(jnp.bfloat16)
    unit_query, factor_query = normalize(queries)
    unit_key, factor_key = normalize(key_rows)
    query_rot = rotary(unit_query * gain_q, position, 1.0).astype(jnp.bfloat16)
    key_rot = rotary(unit_key * gain_k, position, 1.0)[:, 0, :].astype(jnp.bfloat16)
    scores = batched('qhd,kd->hqk', query_rot, key_rot) * SCALE
    expo = jnp.where(allowed[None], jnp.exp(scores), 0.0)
    denom = lax.optimization_barrier(jnp.sum(expo, axis=-1, keepdims=True))
    logsum = jnp.log(denom)
    probs = (expo / denom).astype(jnp.bfloat16)
    mixed = batched('hqk,kd->qhd', probs, value_rows).reshape(count, heads * head_size).astype(jnp.bfloat16)
    return (mixed, (unit_query, factor_query, unit_key, factor_key, query_rot, key_rot, value_rows, logsum))

def attention_backward(d_mixed, saved, gain_q, gain_k, position, allowed):
    unit_query, factor_query, unit_key, factor_key, query_rot, key_rot, value_rows, logsum = saved
    count, heads, head_size = unit_query.shape
    d_heads = d_mixed.reshape(count, heads, head_size)
    scores = batched('qhd,kd->hqk', query_rot, key_rot) * SCALE
    probs_back = jnp.where(allowed[None], jnp.exp(scores - logsum), 0.0)
    d_probs = batched('qhd,kd->hqk', d_heads, value_rows)
    row_dot = lax.optimization_barrier(jnp.sum(probs_back * d_probs, axis=-1, keepdims=True))
    d_scores = (probs_back * (d_probs - row_dot) * SCALE).astype(jnp.bfloat16)
    d_values = batched('hqk,qhd->kd', probs_back.astype(jnp.bfloat16), d_heads).astype(jnp.bfloat16)
    d_query_rot = batched('hqk,kd->qhd', d_scores, key_rot)
    d_key_rot = batched('hqk,qhd->kd', d_scores, query_rot)
    d_unit_query = rotary(d_query_rot, position, -1.0)
    d_unit_key = rotary(d_key_rot[:, None, :], position, -1.0)
    grad_qgain = lax.optimization_barrier(jnp.sum(d_unit_query * unit_query, axis=(0, 1)))
    grad_kgain = lax.optimization_barrier(jnp.sum(d_unit_key * unit_key, axis=(0, 1)))
    d_queries = norm_back(d_unit_query * gain_q, unit_query, factor_query).reshape(count, heads * head_size).astype(jnp.bfloat16)
    d_keys = norm_back(d_unit_key * gain_k, unit_key, factor_key)[:, 0, :].astype(jnp.bfloat16)
    return (d_queries, d_keys, d_values, grad_qgain, grad_kgain)

def layer(tok_block, cot_block, labels, id_block, weights):
    query_full, key_full, value_full, output_full, ffn_rows, g_attn_pre, g_attn_post, g_query, g_key, g_ffn_pre, g_ffn_post = weights
    width = tok_block.shape[1]
    position, allowed = layout_of(labels)
    live = (id_block >= 0).astype(jnp.float32)[:, None]
    inputs = tok_block.astype(jnp.float32)
    unit_in, factor_in = normalize(inputs)
    attn_in = (unit_in * g_attn_pre).astype(jnp.bfloat16)
    mixed, saved = attention_forward(attn_in, query_full, key_full, value_full, g_query, g_key, position, allowed)
    attn_raw = product(mixed, output_full)
    unit_post, factor_post = normalize(attn_raw)
    resid = inputs + unit_post * g_attn_post
    unit_ffn, factor_ffn = normalize(resid)
    ffn_in = (unit_ffn * g_ffn_pre).astype(jnp.bfloat16)
    gate_block = ffn_rows[:, :width]
    up_block = ffn_rows[:, width:2 * width]
    down_block = ffn_rows[:, 2 * width:]
    gate = cross_cols(ffn_in, gate_block)
    up_rows = cross_cols(ffn_in, up_block)
    gelu_val, gelu_slope = gelu_pair(gate)
    hidden = (gelu_val * up_rows).astype(jnp.bfloat16)
    ffn_raw = product(hidden, down_block)
    unit_last, factor_last = normalize(ffn_raw)
    out_rows = resid + unit_last * g_ffn_post
    activations = (live * out_rows).astype(jnp.bfloat16)
    cot_live = cot_block.astype(jnp.float32) * live
    grad_ffn_post = lax.optimization_barrier(jnp.sum(cot_live * unit_last, axis=0))
    d_ffn_raw = norm_back(cot_live * g_ffn_post, unit_last, factor_last).astype(jnp.bfloat16)
    d_hidden = cross_cols(d_ffn_raw, down_block)
    d_gate = (d_hidden * up_rows * gelu_slope).astype(jnp.bfloat16)
    d_up = (d_hidden * gelu_val).astype(jnp.bfloat16)
    grad_ffn = jnp.concatenate([cross_rows(d_gate, ffn_in), cross_rows(d_up, ffn_in), cross_rows(hidden, d_ffn_raw)], axis=1)
    d_ffn_in = product(d_gate, gate_block) + product(d_up, up_block)
    grad_ffn_pre = lax.optimization_barrier(jnp.sum(d_ffn_in * unit_ffn, axis=0))
    d_resid = cot_live + norm_back(d_ffn_in * g_ffn_pre, unit_ffn, factor_ffn)
    grad_attn_post = lax.optimization_barrier(jnp.sum(d_resid * unit_post, axis=0))
    d_attn_raw = norm_back(d_resid * g_attn_post, unit_post, factor_post).astype(jnp.bfloat16)
    grad_output = cross_rows(mixed, d_attn_raw)
    d_mixed = cross_cols(d_attn_raw, output_full).astype(jnp.bfloat16)
    d_queries, d_keys, d_values, grad_qgain, grad_kgain = attention_backward(d_mixed, saved, g_query, g_key, position, allowed)
    grad_query = cross_rows(attn_in, d_queries)
    grad_key = cross_rows(attn_in, d_keys)
    grad_value = cross_rows(attn_in, d_values)
    d_attn_in = cross_cols(d_queries, query_full) + cross_cols(d_keys, key_full) + cross_cols(d_values, value_full)
    grad_attn_pre = lax.optimization_barrier(jnp.sum(d_attn_in * unit_in, axis=0))
    token_grad = d_resid + norm_back(d_attn_in * g_attn_pre, unit_in, factor_in)
    grads = (grad_query, grad_key, grad_value, grad_output, grad_ffn, grad_attn_pre, grad_attn_post, grad_qgain, grad_kgain, grad_ffn_pre, grad_ffn_post)
    return (activations, token_grad, grads)

def reference(tokens, cotangent, seq_ids, w_query, w_key, w_value, w_output, ffn_rows, gain_attn_pre, gain_attn_post, gain_query, gain_key, gain_ffn_pre, gain_ffn_post):
    devices = ROWS // CAP
    group = math.gcd(devices, 16)
    span = group * CAP
    blocks = ROWS // span
    width = tokens.shape[1]
    gains = tuple((item.astype(jnp.float32) for item in (gain_attn_pre, gain_attn_post, gain_query, gain_key, gain_ffn_pre, gain_ffn_post)))
    weights = (w_query, w_key, w_value, w_output, ffn_rows) + gains
    shapes = [w_query.shape, w_key.shape, w_value.shape, w_output.shape, ffn_rows.shape, gain_attn_pre.shape, gain_attn_post.shape, gain_query.shape, gain_key.shape, gain_ffn_pre.shape, gain_ffn_post.shape]
    initial = tuple((jnp.zeros(shape, jnp.float32) for shape in shapes))

    def step(carry, pieces):
        block_index, tok_block, cot_block, id_block = pieces
        device = block_index * group + jnp.arange(span, dtype=jnp.int32) // CAP
        labels = jnp.where(id_block >= 0, device * CAP + id_block, -1 - device).astype(jnp.int32)
        activ, tgrad, grads = layer(tok_block, cot_block, labels, id_block, weights)
        return (tuple((total + part_sum for total, part_sum in zip(carry, grads))), (activ, tgrad))
    inputs = (jnp.arange(blocks, dtype=jnp.int32), tokens.reshape(blocks, span, width), cotangent.reshape(blocks, span, width), seq_ids.reshape(blocks, span))
    totals, stacked = lax.scan(step, initial, inputs)
    activations = stacked[0].reshape(ROWS, width)
    token_grad = stacked[1].reshape(ROWS, width)
    return (activations, token_grad, totals[0], totals[1], totals[2], totals[3], totals[4], totals[5], totals[6], totals[7], totals[8], totals[9], totals[10])
```

```python
import jax
import jax.numpy as jnp
from jax import lax
from jax.sharding import PartitionSpec as P

EPS = 1e-06
SCALE = 0.0625
BASE = 10000.0
CUBIC = 0.044715
ROOT_TERM = 0.7978845608028654
F32 = jnp.float32
BF16 = jnp.bfloat16


def normalize(values):
    factor = lax.rsqrt(jnp.mean(values * values, axis=-1, keepdims=True) + EPS)
    return (values * factor, factor)


def norm_back(incoming, unit, factor):
    return factor * (incoming - unit * jnp.mean(incoming * unit, axis=-1, keepdims=True))


def gelu_pair(values):
    tangent = jnp.tanh(ROOT_TERM * (values + CUBIC * values * values * values))
    result = 0.5 * values * (1.0 + tangent)
    slope = 0.5 * (1.0 + tangent) + 0.5 * values * (1.0 - tangent * tangent) * ROOT_TERM * (
        1.0 + 3.0 * CUBIC * values * values
    )
    return (result, slope)


def rotary_tables(position, size):
    half = size // 2
    ladder = jnp.arange(half, dtype=F32) * (2.0 / size)
    freq = jnp.power(jnp.float32(BASE), -ladder)
    angle = position.astype(F32)[:, None] * freq[None, :]
    return (jnp.cos(angle), jnp.sin(angle))


def rotary(values, cosine, sine):
    half = values.shape[-1] // 2
    first = values[..., :half]
    second = values[..., half:]
    cosine = cosine[:, None, :]
    sine = sine[:, None, :]
    return jnp.concatenate(
        [first * cosine - second * sine, second * cosine + first * sine], axis=-1
    )


def layout_of(labels):
    count = labels.shape[0]
    index = jnp.arange(count, dtype=jnp.int32)
    same = labels[:, None] == labels[None, :]
    earlier = index[None, :] < index[:, None]
    position = jnp.sum(jnp.where(same & earlier, 1, 0), axis=1).astype(jnp.int32)
    allowed = same & (index[None, :] <= index[:, None])
    return (position, allowed)


def product(left, right):
    return jnp.dot(left, right, preferred_element_type=F32)


def cross_rows(left, right):
    return lax.dot_general(left, right, (((0,), (0,)), ((), ())), preferred_element_type=F32)


def cross_cols(left, right):
    return lax.dot_general(left, right, (((1,), (1,)), ((), ())), preferred_element_type=F32)


def batched(form, left, right):
    return jnp.einsum(form, left, right, preferred_element_type=F32)


class Links:
    def __init__(self, mesh):
        self.dp = mesh.shape["dp"]
        self.fsdp = mesh.shape["fsdp"]
        assert self.dp & (self.dp - 1) == 0 and self.fsdp & (self.fsdp - 1) == 0
        count = self.dp.bit_length() - 1
        self.bits = [1] + [1 << i for i in range(count - 1, 0, -1)] if count else []
        self.wires = self.bits[1:]
        self.total = self.dp * self.fsdp

    def swap(self, value, axis, offset):
        size = self.dp if axis == "dp" else self.fsdp
        return lax.ppermute(value, axis, [(i, i ^ offset) for i in range(size)])

    def lift(self, value):
        return value.reshape((1,) * (len(self.bits) + 1) + value.shape)

    def gather_line(self, value):
        parts = [value] + [self.swap(value, "fsdp", k) for k in range(1, self.fsdp)]
        return jnp.concatenate(parts, axis=len(self.bits))

    def gather_bit(self, value, bit):
        return jnp.concatenate([value, self.swap(value, "dp", bit)], axis=self.bits.index(bit))

    def gather_plane(self, value, order):
        for bit in order:
            value = self.gather_bit(value, bit)
        return value

    def orders(self):
        return (self.wires, self.wires[::-1])

    def reduce_bit(self, value, bit):
        axis = self.bits.index(bit)
        keep = lax.slice_in_dim(value, 0, 1, axis=axis)
        send = lax.slice_in_dim(value, 1, 2, axis=axis).astype(BF16)
        return keep.astype(F32) + self.swap(send, "dp", bit).astype(F32)

    def reduce_line(self, value):
        axis = len(self.bits)
        total = lax.slice_in_dim(value, 0, 1, axis=axis).astype(F32)
        for k in range(1, self.fsdp):
            send = lax.slice_in_dim(value, k, k + 1, axis=axis).astype(BF16)
            total = total + self.swap(send, "fsdp", k).astype(F32)
        return total

    def owners(self):
        shape = (2,) * len(self.bits) + (self.fsdp,)
        index = jnp.arange(self.total, dtype=jnp.int32)
        line = index % self.fsdp
        rest = index // self.fsdp
        offset = jnp.zeros_like(index)
        for bit in self.bits[::-1]:
            offset = offset + (rest % 2) * bit
            rest = rest // 2
        return (lax.axis_index("dp") ^ offset) * self.fsdp + (lax.axis_index("fsdp") ^ line)


def one_hot_rows(owners, rows, padded):
    inner = jnp.arange(padded, dtype=jnp.int32)
    target = jnp.where(inner[None, :] < rows, owners[:, None] * rows + inner[None, :], -1)
    size = owners.shape[0] * rows
    return (jnp.arange(size, dtype=jnp.int32)[:, None] == target.reshape(-1)[None, :]).astype(BF16)


def split3(value):
    high = value.astype(BF16)
    rest = value - high.astype(F32)
    middle = rest.astype(BF16)
    low = (rest - middle.astype(F32)).astype(BF16)
    return (high, middle, low)


def make_local(mesh):
    links = Links(mesh)

    def local(
        tokens,
        cotangent,
        seq_ids,
        w_query,
        w_key,
        w_value,
        w_output,
        ffn_rows,
        gain_attn_pre,
        gain_attn_post,
        gain_query,
        gain_key,
        gain_ffn_pre,
        gain_ffn_post,
    ):
        count, width = tokens.shape
        rows = w_query.shape[0]
        q_width = w_query.shape[1]
        head_size = w_key.shape[1]
        heads = q_width // head_size
        out_rows_n = w_output.shape[0]
        padded = (rows + 8) // 8 * 8
        n = links.total
        small = gain_query.shape[0]

        packed = jnp.concatenate([w_query, w_key, w_value], axis=1)
        wide = packed.shape[1]
        gain_row = jnp.concatenate(
            [gain_attn_pre, gain_attn_post, gain_ffn_pre, gain_ffn_post, gain_query, gain_key]
        )
        gain_n = gain_row.shape[0]
        tail = jnp.pad(gain_row[None, :], ((0, padded - rows - 1), (0, wide - gain_n)))
        packed = jnp.concatenate([packed, tail], axis=0)
        half = wide // 2
        line = links.gather_line(links.lift(packed))
        order_a, order_b = links.orders()
        first = links.gather_plane(line[..., :half], order_a)
        second = links.gather_plane(line[..., half:], order_b)
        first = links.gather_bit(first, 1).reshape(n * padded, half)
        second = links.gather_bit(second, 1).reshape(n * padded, wide - half)
        out_line = links.gather_line(links.lift(w_output))
        cut = (width // 256) * 128
        out_a = links.gather_bit(links.gather_plane(out_line[..., :cut], order_a), 1)
        out_b = links.gather_bit(links.gather_plane(out_line[..., cut:], order_b), 1)
        output_full = jnp.concatenate([out_a, out_b], axis=-1).reshape(n * out_rows_n, width)

        gate_own = ffn_rows[:, :width]
        up_own = ffn_rows[:, width : 2 * width]
        down_own = ffn_rows[:, 2 * width :]
        gate_full = links.gather_bit(links.gather_plane(links.lift(gate_own), order_a), 1)
        up_full = links.gather_bit(links.gather_plane(links.lift(up_own), order_b), 1)
        down_a = links.gather_bit(
            links.gather_plane(links.lift(down_own[:, :cut]), order_a), 1
        )
        down_b = links.gather_bit(
            links.gather_plane(links.lift(down_own[:, cut:]), order_b), 1
        )
        units = links.dp * ffn_rows.shape[0]
        gate_full = gate_full.reshape(units, width)
        up_full = up_full.reshape(units, width)
        down_full = jnp.concatenate([down_a, down_b], axis=-1).reshape(units, width)

        owners = links.owners()
        gain_blocks = first.reshape(n, padded, half)[:, rows, :gain_n]
        spread_wide = (
            owners[:, None] == (jnp.arange(width, dtype=jnp.int32) // rows)[None, :]
        ).astype(BF16)
        spread_head = (
            owners[:, None] == (jnp.arange(head_size, dtype=jnp.int32) // small)[None, :]
        ).astype(BF16)
        lane = jnp.arange(gain_n, dtype=jnp.int32)[:, None]
        inner_wide = (jnp.arange(width, dtype=jnp.int32) % rows)[None, :]
        inner_head = (jnp.arange(head_size, dtype=jnp.int32) % small)[None, :]
        masks = [lane == inner_wide + k * rows for k in range(4)] + [
            lane == inner_head + 4 * rows + k * small for k in range(2)
        ]
        wide_gains = cross_rows(gain_blocks, spread_wide)
        head_gains = cross_rows(gain_blocks, spread_head)
        g_attn_pre, g_attn_post, g_ffn_pre, g_ffn_post = (
            jnp.sum(jnp.where(masks[k], wide_gains, 0.0), axis=0) for k in range(4)
        )
        g_query, g_key = (
            jnp.sum(jnp.where(masks[4 + k], head_gains, 0.0), axis=0) for k in range(2)
        )

        position, allowed = layout_of(seq_ids)
        cosine, sine = rotary_tables(position, head_size)
        live = (seq_ids >= 0).astype(F32)[:, None]
        inputs = tokens.astype(F32)
        unit_in, factor_in = normalize(inputs)
        attn_in = (unit_in * g_attn_pre).astype(BF16)
        choose_in = one_hot_rows(owners, rows, padded)
        choose_out = one_hot_rows(owners, out_rows_n, out_rows_n)
        attn_sel = product(attn_in, choose_in).astype(BF16)
        projected = jnp.concatenate(
            [product(attn_sel, first), product(attn_sel, second)], axis=1
        )
        queries = projected[:, :q_width].reshape(count, heads, head_size)
        key_rows = projected[:, q_width : q_width + head_size][:, None, :]
        value_rows = projected[:, q_width + head_size :].astype(BF16)
        unit_query, factor_query = normalize(queries)
        unit_key, factor_key = normalize(key_rows)
        query_rot = rotary(unit_query * g_query, cosine, sine).astype(BF16)
        key_rot = rotary(unit_key * g_key, cosine, sine)[:, 0, :].astype(BF16)
        scores = batched("qhd,kd->hqk", query_rot, key_rot) * SCALE
        expo = jnp.where(allowed[None], jnp.exp(scores), 0.0)
        denom = jnp.sum(expo, axis=-1, keepdims=True)
        logsum = jnp.log(denom)
        probs = (expo / denom).astype(BF16)
        mixed = (
            batched("hqk,kd->qhd", probs, value_rows).reshape(count, q_width).astype(BF16)
        )
        mixed_sel = product(mixed, choose_out).astype(BF16)
        attn_raw = product(mixed_sel, output_full)
        unit_post, factor_post = normalize(attn_raw)
        resid = inputs + unit_post * g_attn_post
        unit_ffn, factor_ffn = normalize(resid)
        ffn_in = (unit_ffn * g_ffn_pre).astype(BF16)

        rows_in = [ffn_in] + [links.swap(ffn_in, "fsdp", k) for k in range(1, links.fsdp)]
        saved = []
        ffn_raw = None
        parts = []
        for k in list(range(1, links.fsdp)) + [0]:
            gate = cross_cols(rows_in[k], gate_full)
            up = cross_cols(rows_in[k], up_full)
            gelu_val, gelu_slope = gelu_pair(gate)
            hidden = (gelu_val * up).astype(BF16)
            part = product(hidden, down_full)
            if k:
                part = links.swap(part.astype(BF16), "fsdp", k).astype(F32)
            parts.append(part)
            saved.append((k, gelu_val, up * gelu_slope))
        ffn_raw = sum(parts[1:], parts[0])
        unit_last, factor_last = normalize(ffn_raw)
        out_rows = resid + unit_last * g_ffn_post
        activations = (live * out_rows).astype(BF16)

        cot_live = cotangent.astype(F32) * live
        grad_ffn_post = jnp.sum(cot_live * unit_last, axis=0)
        d_ffn_raw = norm_back(cot_live * g_ffn_post, unit_last, factor_last).astype(BF16)
        rows_back = [d_ffn_raw] + [links.swap(d_ffn_raw, "fsdp", k) for k in range(1, links.fsdp)]
        parts = []
        for k, gelu_val, up_slope in saved:
            d_hidden = cross_cols(rows_back[k], down_full)
            d_gate = (d_hidden * up_slope).astype(BF16)
            d_up = (d_hidden * gelu_val).astype(BF16)
            part = product(d_gate, gate_full) + product(d_up, up_full)
            if k:
                part = links.swap(part.astype(BF16), "fsdp", k).astype(F32)
            parts.append(part)
        d_ffn_in = sum(parts[1:], parts[0])

        def everyone(blocks):
            block = links.lift(jnp.stack(blocks, axis=0))
            block = block.reshape(block.shape[:-4] + block.shape[-3:])
            left = links.gather_bit(links.gather_plane(block[..., :cut], order_a), 1)
            right = links.gather_bit(links.gather_plane(block[..., cut:], order_b), 1)
            return jnp.concatenate([left, right], axis=-1).reshape(n * count, width)

        all_in = everyone(rows_in)
        own_gate = cross_cols(gate_own, all_in)
        own_up = cross_cols(up_own, all_in)
        own_gelu, own_slope = gelu_pair(own_gate)
        own_hidden = (own_gelu * own_up).astype(BF16)
        own_up_slope = own_up * own_slope
        all_back = everyone(rows_back)
        own_d_hidden = cross_cols(down_own, all_back)
        own_d_gate = (own_d_hidden * own_up_slope).astype(BF16)
        own_d_up = (own_d_hidden * own_gelu).astype(BF16)
        grad_ffn = jnp.concatenate(
            [product(own_d_gate, all_in), product(own_d_up, all_in), product(own_hidden, all_back)],
            axis=1,
        )

        grad_ffn_pre = jnp.sum(d_ffn_in * unit_ffn, axis=0)
        d_resid = cot_live + norm_back(d_ffn_in * g_ffn_pre, unit_ffn, factor_ffn)
        grad_attn_post = jnp.sum(d_resid * unit_post, axis=0)
        d_attn_raw = norm_back(d_resid * g_attn_post, unit_post, factor_post).astype(BF16)
        grad_output = cross_rows(mixed_sel, d_attn_raw)
        d_mixed_sel = cross_cols(d_attn_raw, output_full).astype(BF16)
        d_mixed = cross_cols(d_mixed_sel, choose_out).astype(BF16)
        d_heads = d_mixed.reshape(count, heads, head_size)
        probs_back = jnp.where(allowed[None], jnp.exp(scores - logsum), 0.0)
        d_probs = batched("qhd,kd->hqk", d_heads, value_rows)
        row_dot = jnp.sum(probs_back * d_probs, axis=-1, keepdims=True)
        d_scores = (probs_back * (d_probs - row_dot) * SCALE).astype(BF16)
        d_values = batched("hqk,qhd->kd", probs_back.astype(BF16), d_heads).astype(BF16)
        d_query_rot = batched("hqk,kd->qhd", d_scores, key_rot)
        d_key_rot = batched("hqk,qhd->kd", d_scores, query_rot)
        d_unit_query = rotary(d_query_rot, cosine, -sine)
        d_unit_key = rotary(d_key_rot[:, None, :], cosine, -sine)
        grad_qgain = jnp.sum(d_unit_query * unit_query, axis=(0, 1))
        grad_kgain = jnp.sum(d_unit_key * unit_key, axis=(0, 1))
        d_queries = (
            norm_back(d_unit_query * g_query, unit_query, factor_query)
            .reshape(count, q_width)
            .astype(BF16)
        )
        d_keys = norm_back(d_unit_key * g_key, unit_key, factor_key)[:, 0, :].astype(BF16)
        d_projected = jnp.concatenate([d_queries, d_keys, d_values], axis=1)
        d_attn_sel = cross_cols(d_projected[:, :half], first) + cross_cols(
            d_projected[:, half:], second
        )
        high, middle, low = split3(d_attn_sel)
        d_attn_in = (
            cross_cols(high, choose_in) + cross_cols(middle, choose_in) + cross_cols(low, choose_in)
        )
        grad_attn_pre = jnp.sum(d_attn_in * unit_in, axis=0)
        token_grad = d_resid + norm_back(d_attn_in * g_attn_pre, unit_in, factor_in)

        wide_grads = (grad_attn_pre, grad_attn_post, grad_ffn_pre, grad_ffn_post)
        head_grads = (grad_qgain, grad_kgain)
        wide_field = sum(
            jnp.where(masks[k], wide_grads[k].astype(BF16)[None, :], 0) for k in range(4)
        )
        head_field = sum(
            jnp.where(masks[4 + k], head_grads[k].astype(BF16)[None, :], 0) for k in range(2)
        )
        gain_field = cross_cols(spread_wide, wide_field) + cross_cols(spread_head, head_field)

        def owned(value, order):
            value = links.reduce_bit(value, 1)
            for bit in order[::-1]:
                value = links.reduce_bit(value, bit)
            return links.reduce_line(value)

        lead = (2,) * len(links.bits) + (links.fsdp,)
        grad_first = cross_rows(attn_sel, d_projected[:, :half]).reshape(n, padded, half)
        grad_first = grad_first.at[:, rows, :gain_n].set(gain_field)
        grad_second = cross_rows(attn_sel, d_projected[:, half:])
        sum_first = owned(grad_first.reshape(lead + (padded, half)), order_a)
        sum_second = owned(grad_second.reshape(lead + (padded, wide - half)), order_b)
        sum_first = sum_first.reshape(padded, half)
        sum_second = sum_second.reshape(padded, wide - half)
        sum_wide = jnp.concatenate([sum_first[:rows], sum_second[:rows]], axis=1)
        grad_output = grad_output.reshape(lead + (out_rows_n, width))
        sum_out_a = owned(grad_output[..., :cut], order_a).reshape(out_rows_n, cut)
        sum_out_b = owned(grad_output[..., cut:], order_b).reshape(out_rows_n, width - cut)
        sum_out = jnp.concatenate([sum_out_a, sum_out_b], axis=1)
        sums = sum_first[rows]
        return (
            activations,
            token_grad,
            sum_wide[:, :q_width],
            sum_wide[:, q_width : q_width + head_size],
            sum_wide[:, q_width + head_size :],
            sum_out,
            grad_ffn,
            sums[:rows],
            sums[rows : 2 * rows],
            sums[4 * rows : 4 * rows + small],
            sums[4 * rows + small : 4 * rows + 2 * small],
            sums[2 * rows : 3 * rows],
            sums[3 * rows : 4 * rows],
        )

    return local


def solution(mesh):
    both = ("dp", "fsdp")
    matrix = P(both, None)
    vector = P(both)
    return jax.shard_map(
        make_local(mesh),
        mesh=mesh,
        in_specs=(matrix, matrix, vector) + (matrix,) * 5 + (vector,) * 6,
        out_specs=(matrix,) * 7 + (vector,) * 6,
        check_vma=False,
    )
```
